32 devices in a mesh: groups: 1, ctx: 32 (over z, y, x, core).
Axes of the slice: x: 2, y: 2, z: 4, core: 2. Of those that a mesh axis runs over, the one named last changes fastest.
Arguments:
- prefill_query: bfloat16 [1024, 32, 576], P('groups', 'ctx'), may hold values from -1000 to 1000
- prefill_latent: bfloat16 [1024, 576], P(('groups', 'ctx')), may hold values from -6 to 6
- decode_query: bfloat16 [2, 32, 576], P('groups'), may hold values from -1000 to 1000
- cache: bfloat16 [2, 16384, 576], P('groups', 'ctx'), may hold values from -6 to 6
- lengths: int32 [2], P('groups'), may hold values from 2049 to 16384
- page_table: int32 [64, 2], P('groups'), may hold values from 0 to 31, as said below
Outputs:
- prefill_out: bfloat16 [1024, 32, 512], P('groups', 'ctx')
- decode_out: bfloat16 [2, 32, 512], P('groups', 'ctx')
The draws below stay inside these ranges and needn't reach their ends.
Inputs may be any that keep to these rules, and one draw needn't show every extreme that they name: `page_table`: row p names the device (column 0, below 32) and the pool slot (column 1, below 16) that take latent page p; no two rows name the same pair.
All inputs are finite; a program needn't handle non-finite values.
Results may differ from the reference program's by a relative error of at most 0.0049.
Values may be sent and summed in bfloat16 or wider, within the bound.
No kernel may reach another device: no remote copies, remote signals or barrier semaphores. Data moves between devices by JAX's collectives and lax.ppermute only.
A program may use at most 64 MiB of HBM per device.

```python
import jax
import jax.numpy as jnp
from jax import lax

D_LAT = 512
D_ROPE = 64
PAGE = 16
POOL = 16
SPAN = 1024
REQ = 2
HEADS = 32
CTXLEN = 16384
NPAGES = 64
N_CTX = 32


SCALE = 192.0 ** (-0.5)


def cache_block(key, request, block):
    sub_key = jax.random.fold_in(jax.random.fold_in(jax.random.fold_in(key, 501), request), block)
    raw = jax.random.normal(sub_key, (64, D_LAT + D_ROPE), jnp.float32)
    return jnp.clip(raw, -6.0, 6.0).astype(jnp.bfloat16).astype(jnp.float32)


def cache_row(key, request, position):
    return cache_block(key, request, position // 64)[position % 64]


def latent_matrix(key):
    raw = jax.random.normal(jax.random.fold_in(key, 502), (SPAN, D_LAT + D_ROPE), jnp.float32)
    return jnp.clip(raw, -6.0, 6.0).astype(jnp.bfloat16).astype(jnp.float32)


def aligned(first, second, strength):
    self_first = jnp.sum(first * first, axis=-1)
    self_second = jnp.sum(second * second, axis=-1)
    cross = jnp.sum(first * second, axis=-1)
    coefficient = (strength * (self_first - cross) - 2.0 / SCALE) / (self_second - cross)
    return strength[..., None] * first + coefficient[..., None] * second


def strength_table():
    return jnp.array([3.0, 5.0, 8.0], jnp.float32) * (576.0 / (D_LAT + D_ROPE))


def prefill_built(key):
    latent = latent_matrix(key)
    picked = HEADS // 16
    row_index = jnp.arange(SPAN)[:, None]
    head_index = jnp.arange(picked)[None, :]
    other = jax.random.randint(jax.random.fold_in(key, 512), (SPAN, picked), 0, SPAN) % jnp.maximum(row_index, 1)
    strength = strength_table()[(head_index + row_index) % 3]
    first = latent[jnp.broadcast_to(row_index, (SPAN, picked))]
    second = latent[other]
    built = aligned(first, second, strength)
    chosen = jnp.broadcast_to(row_index % 64 == 63, (SPAN, picked))
    return (built, chosen)


def decode_built(key):
    picked = HEADS // 16
    reach = CTXLEN // 8
    first_pos = jax.random.randint(jax.random.fold_in(key, 522), (REQ, picked), 0, reach)
    step_pos = jax.random.randint(jax.random.fold_in(key, 523), (REQ, picked), 1, reach)
    second_pos = (first_pos + step_pos) % reach
    request_index = jnp.broadcast_to(jnp.arange(REQ)[:, None], (REQ, picked))
    head_index = jnp.arange(picked)[None, :]
    row_fetch = jax.vmap(jax.vmap(lambda request, position: cache_row(key, request, position)))
    first = row_fetch(request_index, first_pos)
    second = row_fetch(request_index, second_pos)
    strength = strength_table()[(head_index + request_index) % 3]
    return aligned(first, second, strength)


def draw_cache(key, part):
    blocks = CTXLEN // 64
    full = jax.vmap(lambda request: jax.vmap(lambda block: cache_block(key, request, block))(jnp.arange(blocks)))(jnp.arange(REQ))
    return full.reshape(REQ, CTXLEN, D_LAT + D_ROPE).astype(jnp.bfloat16)


def draw_prefill_latent(key, part):
    return latent_matrix(key).astype(jnp.bfloat16)


def draw_prefill_query(key, part):
    width = D_LAT + D_ROPE
    plain = 2.0 * jnp.clip(jax.random.normal(jax.random.fold_in(key, 513), (SPAN, HEADS, width), jnp.float32), -6.0, 6.0)
    built, chosen = prefill_built(key)
    query = plain.at[:, ::16, :].set(jnp.where(chosen[..., None], built, plain[:, ::16, :]))
    return jnp.clip(query, -1000.0, 1000.0).astype(jnp.bfloat16)


def draw_decode_query(key, part):
    width = D_LAT + D_ROPE
    plain = 2.0 * jnp.clip(jax.random.normal(jax.random.fold_in(key, 524), (REQ, HEADS, width), jnp.float32), -6.0, 6.0)
    query = plain.at[:, ::16, :].set(decode_built(key))
    return jnp.clip(query, -1000.0, 1000.0).astype(jnp.bfloat16)


def draw_page_table(key, part):
    order = jax.random.permutation(jax.random.fold_in(key, 531), N_CTX * POOL)[:NPAGES]
    return jnp.stack([order // POOL, order % POOL], axis=1).astype(jnp.int32)


def setup_inputs(seed: int = 0, part: int = 0) -> dict:
    keys = jax.random.split(jax.random.key(seed), 7)
    own_keys = jax.random.split(jax.random.fold_in(keys[6], part), 7)
    prefill_query = draw_prefill_query(jax.random.fold_in(jax.random.fold_in(keys[6], part), 71), part)
    prefill_latent = draw_prefill_latent(jax.random.fold_in(jax.random.fold_in(keys[6], part), 71), part)
    decode_query = draw_decode_query(jax.random.fold_in(jax.random.fold_in(keys[6], part), 71), part)
    cache = draw_cache(jax.random.fold_in(jax.random.fold_in(keys[6], part), 71), part)
    lengths = jax.random.randint(own_keys[4], (REQ,), CTXLEN // 8 + 1, CTXLEN + 1).astype(jnp.int32)
    page_table = draw_page_table(jax.random.fold_in(jax.random.fold_in(keys[6], part), 71), part)
    return dict(prefill_query=prefill_query, prefill_latent=prefill_latent, decode_query=decode_query, cache=cache, lengths=lengths, page_table=page_table)


SCALE = 192.0 ** -0.5
NEG = -1.0e30


def softmax_values(scores, allowed, values):
    masked = jnp.where(allowed, scores, NEG)
    top_score = jnp.max(masked, axis=-1, keepdims=True)
    weights = jnp.where(allowed, jnp.exp(scores - top_score), 0.0)
    weight_sum = jnp.sum(weights, axis=-1, keepdims=True)
    mixed = jnp.dot(weights.astype(jnp.bfloat16), values, preferred_element_type=jnp.float32)
    return mixed / weight_sum


def reference(prefill_query, prefill_latent, decode_query, cache, lengths, page_table):
    latent_values = prefill_latent[:, :D_LAT]
    causal = jnp.arange(SPAN, dtype=jnp.int32)[:, None] >= jnp.arange(SPAN, dtype=jnp.int32)[None, :]

    def one_head(queries):
        scores = jnp.dot(queries, prefill_latent.T, preferred_element_type=jnp.float32) * SCALE
        return softmax_values(scores, causal, latent_values).astype(jnp.bfloat16)

    per_head = lax.map(one_head, jnp.swapaxes(prefill_query, 0, 1))
    prefill_out = jnp.swapaxes(per_head, 0, 1)

    page_request = (page_table[:, 0] * POOL + page_table[:, 1]) % REQ
    token_request = jnp.repeat(page_request, PAGE)
    positions = jnp.arange(CTXLEN, dtype=jnp.int32)

    def one_request(request):
        queries = decode_query[request]
        rows_cache = cache[request]
        cache_scores = jnp.dot(queries, rows_cache.T, preferred_element_type=jnp.float32) * SCALE
        page_scores = jnp.dot(queries, prefill_latent.T, preferred_element_type=jnp.float32) * SCALE
        scores = jnp.concatenate([cache_scores, page_scores], axis=1)
        allowed = jnp.concatenate([positions < lengths[request], token_request == request])[None, :]
        values = jnp.concatenate([rows_cache[:, :D_LAT], latent_values], axis=0)
        return softmax_values(scores, allowed, values).astype(jnp.bfloat16)

    decode_out = lax.map(one_request, jnp.arange(REQ, dtype=jnp.int32))
    return prefill_out, decode_out
```

```python
import functools

import jax
import jax.numpy as jnp
from jax import lax
from jax.experimental import pallas as pl
from jax.experimental.pallas import tpu as pltpu
from jax.sharding import PartitionSpec as P

D_LAT = 512
PAGE = 16
POOL = 16
REQ = 2
LANES = 128

SCALE = 192.0 ** (-0.5)
LOG2E = 1.4426950408889634
NEG = -1e30


def bit_orders(n):
    bits = list(range(n.bit_length() - 2, 0, -1))
    swapped = bits[:-2] + bits[:-3:-1]
    return bits, swapped


def permute_bits(rows, n, even_bit, odd_bit):
    pairs = [(i, i ^ (1 << (odd_bit if i & 1 else even_bit))) for i in range(n)]
    return lax.ppermute(rows, "ctx", pairs)


def slot_mask(order, slot):
    mask = 0
    for step, bit in enumerate(order):
        if (slot >> step) & 1:
            mask |= 1 << bit
    return mask


def decode_kernel(table_ref, lengths_ref, query_ref, cache_ref, latent_ref, packed_ref):
    device = lax.axis_index("ctx")
    rows = latent_ref.shape[0]
    length = cache_ref.shape[2]
    heads = query_ref.shape[1]
    first_page = (device * rows) // PAGE
    token = lax.broadcasted_iota(jnp.int32, (1, rows), 1)
    request = jnp.zeros((1, rows), jnp.int32)
    for k in range(max(1, rows // PAGE)):
        owner = table_ref[0, first_page + k]
        slot = table_ref[1, first_page + k]
        request = jnp.where(token // PAGE == k, lax.rem(owner * POOL + slot, REQ), request)
    position = device * length + lax.broadcasted_iota(jnp.int32, (1, length), 1)
    lane = lax.broadcasted_iota(jnp.int32, (heads, LANES), 1)
    latent = latent_ref[...]
    for r in range(REQ):
        query = query_ref[r]
        cache = cache_ref[r]
        live = position < lengths_ref[r]
        mine = request == r
        cache_scores = jnp.dot(query, cache, preferred_element_type=jnp.float32) * SCALE
        page_scores = (
            lax.dot_general(
                query, latent, (((1,), (1,)), ((), ())), preferred_element_type=jnp.float32
            )
            * SCALE
        )
        top = jnp.maximum(
            jnp.max(jnp.where(live, cache_scores, NEG), axis=1, keepdims=True),
            jnp.max(jnp.where(mine, page_scores, NEG), axis=1, keepdims=True),
        )
        cache_weights = jnp.where(live, jnp.exp(cache_scores - top), 0.0)
        page_weights = jnp.where(mine, jnp.exp(page_scores - top), 0.0)
        total = jnp.sum(cache_weights, axis=1, keepdims=True) + jnp.sum(
            page_weights, axis=1, keepdims=True
        )
        mixed = lax.dot_general(
            cache_weights.astype(jnp.bfloat16),
            cache[:D_LAT],
            (((1,), (1,)), ((), ())),
            preferred_element_type=jnp.float32,
        ) + jnp.dot(
            page_weights.astype(jnp.bfloat16),
            latent[:, :D_LAT],
            preferred_element_type=jnp.float32,
        )
        packed_ref[:, r, :D_LAT] = mixed
        packed_ref[:, r, D_LAT:] = jnp.where(lane == 0, top, total)


def prefill_kernel(
    steps, query_ref, own_ref, swap_ref, moved_ref, out_ref, decode_ref, keys, sems
):
    device = lax.axis_index("ctx")
    parity = lax.rem(device, 2)
    span = query_ref.shape[0]
    slots = 1 << steps
    rows = own_ref.shape[0] // slots
    orders = bit_orders(2 * slots)
    copies = []
    for side, ref in enumerate((own_ref, swap_ref)):
        for slot in range(slots):
            even, odd = slot_mask(orders[0], slot), slot_mask(orders[1], slot)
            mask = jnp.where(parity == side, even, odd) if even != odd else even
            owner = device ^ side ^ mask
            copies.append(
                pltpu.make_async_copy(
                    ref.at[pl.ds(slot * rows, rows)],
                    keys.at[pl.ds(pl.multiple_of(owner * rows, rows), rows)],
                    sems.at[side * slots + slot],
                )
            )
    for copy in copies:
        copy.start()

    moved = moved_ref[...]
    tops = moved[:, :, D_LAT : D_LAT + 1]
    totals = moved[:, :, D_LAT + 1 : D_LAT + 2]
    scales = jnp.exp(tops - jnp.max(tops, axis=0, keepdims=True))
    own_out = jnp.sum(moved[:, :, :D_LAT] * scales, axis=0)
    decode_ref[...] = (own_out / jnp.sum(totals * scales, axis=0)).astype(jnp.bfloat16)

    for copy in copies:
        copy.wait()

    block = min(span, 256)
    for start in range(0, span, block):
        stop = start + block
        scores = lax.dot_general(
            query_ref[start:stop],
            keys[:stop],
            (((1,), (1,)), ((), ())),
            preferred_element_type=jnp.float32,
        )
        row = start + lax.broadcasted_iota(jnp.int32, (block, stop), 0)
        column = lax.broadcasted_iota(jnp.int32, (block, stop), 1)
        scores = jnp.where(column <= row, scores, NEG)
        top = jnp.max(scores, axis=1, keepdims=True)
        weights = jnp.exp2((scores - top) * (SCALE * LOG2E))
        total = jnp.sum(weights, axis=1, keepdims=True)
        mixed = jnp.dot(
            weights.astype(jnp.bfloat16),
            keys[:stop, :D_LAT],
            preferred_element_type=jnp.float32,
        )
        out_ref[start:stop] = (mixed / total).astype(jnp.bfloat16)


def shards(n, prefill_query, prefill_latent, decode_query, cache, lengths, page_table):
    span = prefill_query.shape[0]
    width = prefill_latent.shape[1]
    heads = decode_query.shape[1]
    vmem = pl.BlockSpec(memory_space=pltpu.VMEM)
    smem = pl.BlockSpec(memory_space=pltpu.SMEM)
    anywhere = pl.BlockSpec(memory_space=pl.ANY)

    even_bits, odd_bits = bit_orders(n)
    steps = len(even_bits)
    held = prefill_latent
    for even, odd in zip(even_bits, odd_bits):
        held = jnp.concatenate([held, permute_bits(held, n, even, odd)], axis=0)
    swapped = permute_bits(held, n, 0, 0)

    packed = pl.pallas_call(
        decode_kernel,
        out_shape=jax.ShapeDtypeStruct((heads, REQ, D_LAT + LANES), jnp.float32),
        in_specs=[smem, smem, vmem, vmem, vmem],
        out_specs=vmem,
        cost_estimate=pl.CostEstimate(
            flops=4 * cache.size * heads, bytes_accessed=2 * cache.size, transcendentals=0
        ),
        name="decode_part",
    )(page_table.T, lengths, decode_query, jnp.swapaxes(cache, 1, 2), prefill_latent)
    moved = lax.all_to_all(packed, "ctx", split_axis=0, concat_axis=0, tiled=True)

    prefill_out, decode_out = pl.pallas_call(
        functools.partial(prefill_kernel, steps),
        out_shape=(
            jax.ShapeDtypeStruct((span, D_LAT), jnp.bfloat16),
            jax.ShapeDtypeStruct((REQ, D_LAT), jnp.bfloat16),
        ),
        in_specs=[vmem, anywhere, anywhere, vmem],
        out_specs=(vmem, vmem),
        scratch_shapes=[
            pltpu.VMEM((span, width), jnp.bfloat16),
            pltpu.SemaphoreType.DMA((n,)),
        ],
        cost_estimate=pl.CostEstimate(
            flops=4 * span * span * width,
            bytes_accessed=2 * (span * width * 3),
            transcendentals=span * span,
        ),
        name="prefill",
    )(prefill_query.reshape(span, width), held, swapped, moved)
    return prefill_out.reshape(span, 1, D_LAT), decode_out.reshape(REQ, 1, D_LAT)


def solution(mesh):
    in_specs = (
        P("groups", "ctx", None),
        P(("groups", "ctx"), None),
        P("groups", None, None),
        P("groups", "ctx", None),
        P("groups"),
        P("groups", None),
    )
    out_specs = (P("groups", "ctx", None), P("groups", "ctx", None))
    return jax.shard_map(
        functools.partial(shards, mesh.shape["ctx"]),
        mesh=mesh,
        in_specs=in_specs,
        out_specs=out_specs,
        check_vma=False,
    )
```

```python
import functools

import jax
import jax.numpy as jnp
from jax import lax
from jax.experimental import pallas as pl
from jax.experimental.pallas import tpu as pltpu
from jax.sharding import PartitionSpec as P

D_LAT = 512
PAGE = 16
POOL = 16
REQ = 2
LANES = 128

SCALE = 192.0 ** (-0.5)
LOG2E = 1.4426950408889634
NEG = -1e30

VMEM_LIMIT = 8 << 20


def bit_orders(n):
    bits = list(range(n.bit_length() - 2, 0, -1))
    return bits, bits[:-2] + bits[:-3:-1]


def permute_bits(rows, n, even_bit, odd_bit):
    pairs = [(i, i ^ (1 << (odd_bit if i & 1 else even_bit))) for i in range(n)]
    return lax.ppermute(rows, "ctx", pairs)


def decode_kernel(table_ref, lengths_ref, query_ref, cache_ref, latent_ref, packed_ref):
    device = lax.axis_index("ctx")
    rows = latent_ref.shape[0]
    length = cache_ref.shape[2]
    heads = query_ref.shape[1]
    first_page = (device * rows) // PAGE
    token = lax.broadcasted_iota(jnp.int32, (1, rows), 1)
    request = jnp.zeros((1, rows), jnp.int32)
    for k in range(max(1, rows // PAGE)):
        owner = table_ref[0, first_page + k]
        slot = table_ref[1, first_page + k]
        request = jnp.where(token // PAGE == k, lax.rem(owner * POOL + slot, REQ), request)
    position = device * length + lax.broadcasted_iota(jnp.int32, (1, length), 1)
    lane = lax.broadcasted_iota(jnp.int32, (heads, LANES), 1)
    latent = latent_ref[...]
    for r in range(REQ):
        query = query_ref[r]
        cache = cache_ref[r]
        live = position < lengths_ref[r]
        mine = request == r
        cache_scores = jnp.dot(query, cache, preferred_element_type=jnp.float32) * SCALE
        page_scores = (
            lax.dot_general(
                query, latent, (((1,), (1,)), ((), ())), preferred_element_type=jnp.float32
            )
            * SCALE
        )
        top = jnp.maximum(
            jnp.max(jnp.where(live, cache_scores, NEG), axis=1, keepdims=True),
            jnp.max(jnp.where(mine, page_scores, NEG), axis=1, keepdims=True),
        )
        cache_weights = jnp.where(live, jnp.exp(cache_scores - top), 0.0)
        page_weights = jnp.where(mine, jnp.exp(page_scores - top), 0.0)
        total = jnp.sum(cache_weights, axis=1, keepdims=True) + jnp.sum(
            page_weights, axis=1, keepdims=True
        )
        mixed = lax.dot_general(
            cache_weights.astype(jnp.bfloat16),
            cache[:D_LAT],
            (((1,), (1,)), ((), ())),
            preferred_element_type=jnp.float32,
        ) + jnp.dot(
            page_weights.astype(jnp.bfloat16),
            latent[:, :D_LAT],
            preferred_element_type=jnp.float32,
        )
        packed_ref[:, r, :D_LAT] = mixed
        packed_ref[:, r, D_LAT:] = jnp.where(lane == 0, top, total)


def turn_kernel(start, turned_ref, query_ref):
    query_ref[...] = turned_ref[:, start : start + query_ref.shape[0]].T


def turn_query(turned, start, count, params):
    width = turned.shape[0]
    vmem = pl.BlockSpec(memory_space=pltpu.VMEM)
    return pl.pallas_call(
        functools.partial(turn_kernel, start),
        out_shape=jax.ShapeDtypeStruct((count, width), jnp.bfloat16),
        in_specs=[vmem],
        out_specs=vmem,
        compiler_params=params,
        cost_estimate=pl.CostEstimate(
            flops=0, bytes_accessed=4 * count * width, transcendentals=0
        ),
        name="turn_query",
    )(turned)


def place_keys(own_ref, swap_ref, keys, late):
    device = lax.axis_index("ctx")
    parity = lax.rem(device, 2)
    slots, rows, _ = own_ref.shape
    groups = slots // 2
    bits = (groups * 8).bit_length() - 1
    offsets = []
    for side, ref in enumerate((own_ref, swap_ref)):
        odd = parity ^ side
        third = jnp.where(odd == 1, 2, 4)
        fourth = 6 - third
        base = (device & 7) ^ side
        if late:
            base = base ^ fourth
        for half in range(2):
            offsets.append((base ^ third) if half else base)
            place = 2 * side + half
            for t in range(groups):
                mask = 0
                for step in range(bits - 3):
                    if (t >> step) & 1:
                        mask |= 1 << (bits - 4 - step)
                group = (device // 8) ^ mask
                start = pl.multiple_of((group * 4 + place) * rows, rows)
                keys[pl.ds(start, rows)] = ref[half * groups + t]
    column = lax.broadcasted_iota(jnp.int32, (1, 4 * rows), 1)
    token = jnp.zeros((1, 4 * rows), jnp.int32)
    for place, low in enumerate(offsets):
        token = jnp.where(column // rows == place, low * rows + lax.rem(column, rows), token)
    return token


def block_scores(query, keys, token, index, block, columns):
    scores = lax.dot_general(
        query,
        keys[: (index + 1) * columns],
        (((1,), (1,)), ((), ())),
        preferred_element_type=jnp.float32,
    )
    row = lax.broadcasted_iota(jnp.int32, (block, columns), 0)
    diagonal = jnp.where(token <= row, scores[:, index * columns :], NEG)
    if index == 0:
        return diagonal
    return jnp.concatenate([scores[:, : index * columns], diagonal], axis=1)


def early_kernel(most_ref, rest_ref, own_ref, swap_ref, mixed_ref, stats_ref, keys):
    token = place_keys(own_ref, swap_ref, keys, False)
    columns = token.shape[1]
    block = 2 * columns
    lane = lax.broadcasted_iota(jnp.int32, (block, LANES), 1)
    last = most_ref.shape[0] // block
    for index in range(last + 1):
        span = pl.ds(index * block, block)
        query = rest_ref[...] if index == last else most_ref[span]
        scores = block_scores(query, keys, token, index, block, columns)
        top = jnp.max(scores, axis=1, keepdims=True)
        weights = jnp.exp2((scores - top) * (SCALE * LOG2E))
        total = jnp.sum(weights, axis=1, keepdims=True)
        mixed_ref[span] = jnp.dot(
            weights.astype(jnp.bfloat16),
            keys[: (index + 1) * columns, :D_LAT],
            preferred_element_type=jnp.float32,
        )
        stats_ref[span] = jnp.where(lane == 0, top, total)


def late_kernel(
    most_ref,
    rest_ref,
    own_ref,
    swap_ref,
    mixed_ref,
    stats_ref,
    moved_ref,
    out_ref,
    decode_ref,
    keys,
    blocks,
    sems,
):
    token = place_keys(own_ref, swap_ref, keys, True)
    columns = token.shape[1]
    block = 2 * columns
    copies = []
    last = most_ref.shape[0] // block
    for index in range(last + 1):
        span = pl.ds(index * block, block)
        query = rest_ref[...] if index == last else most_ref[span]
        scores = block_scores(query, keys, token, index, block, columns)
        before = stats_ref[span, 0:1]
        top = jnp.maximum(jnp.max(scores, axis=1, keepdims=True), before)
        weights = jnp.exp2((scores - top) * (SCALE * LOG2E))
        factor = jnp.exp2((before - top) * (SCALE * LOG2E))
        total = jnp.sum(weights, axis=1, keepdims=True) + stats_ref[span, 1:2] * factor
        mixed = mixed_ref[span] * factor + jnp.dot(
            weights.astype(jnp.bfloat16),
            keys[: (index + 1) * columns, :D_LAT],
            preferred_element_type=jnp.float32,
        )
        blocks[span] = (mixed / total).astype(jnp.bfloat16)
        copy = pltpu.make_async_copy(blocks.at[span], out_ref.at[span], sems.at[index])
        copy.start()
        copies.append(copy)

    moved = moved_ref[...]
    tops = moved[:, :, D_LAT : D_LAT + 1]
    totals = moved[:, :, D_LAT + 1 : D_LAT + 2]
    scales = jnp.exp(tops - jnp.max(tops, axis=0, keepdims=True))
    own_out = jnp.sum(moved[:, :, :D_LAT] * scales, axis=0)
    decode_ref[...] = (own_out / jnp.sum(totals * scales, axis=0)).astype(jnp.bfloat16)
    for copy in copies:
        copy.wait()


def shards(n, prefill_query, prefill_latent, decode_query, cache, lengths, page_table):
    span = prefill_query.shape[0]
    rows, width = prefill_latent.shape
    heads = decode_query.shape[1]
    vmem = pl.BlockSpec(memory_space=pltpu.VMEM)
    smem = pl.BlockSpec(memory_space=pltpu.SMEM)
    params = pltpu.CompilerParams(vmem_limit_bytes=VMEM_LIMIT)

    even_bits, odd_bits = bit_orders(n)
    held = prefill_latent[None]
    for step, (even, odd) in enumerate(zip(even_bits, odd_bits)):
        received = permute_bits(held, n, even, odd)
        if step < len(even_bits) - 1:
            held = jnp.concatenate([held, received], axis=0)
    held_swap = permute_bits(held, n, 0, 0)
    received_swap = permute_bits(received, n, 0, 0)

    packed = pl.pallas_call(
        decode_kernel,
        out_shape=jax.ShapeDtypeStruct((heads, REQ, D_LAT + LANES), jnp.float32),
        in_specs=[smem, smem, vmem, vmem, vmem],
        out_specs=vmem,
        compiler_params=params,
        cost_estimate=pl.CostEstimate(
            flops=4 * cache.size * heads, bytes_accessed=2 * cache.size, transcendentals=0
        ),
        name="decode_part",
    )(page_table.T, lengths, decode_query, jnp.swapaxes(cache, 1, 2), prefill_latent)
    moved = lax.all_to_all(packed, "ctx", split_axis=0, concat_axis=0, tiled=True)

    turned = jnp.transpose(prefill_query, (1, 2, 0)).reshape(width, span)
    block = 8 * rows
    query_most = turn_query(turned, 0, span - block, params)
    query_rest = turn_query(turned, span - block, block, params)

    cost = pl.CostEstimate(
        flops=2 * span * span * width, bytes_accessed=4 * span * width, transcendentals=0
    )
    keys = pltpu.VMEM((span // 2, width), jnp.bfloat16)
    mixed, stats = pl.pallas_call(
        early_kernel,
        out_shape=(
            jax.ShapeDtypeStruct((span, D_LAT), jnp.float32),
            jax.ShapeDtypeStruct((span, LANES), jnp.float32),
        ),
        in_specs=[vmem] * 4,
        out_specs=(vmem, vmem),
        scratch_shapes=[keys],
        compiler_params=params,
        cost_estimate=cost,
        name="prefill_early",
    )(query_most, query_rest, held, held_swap)
    prefill_out, decode_out = pl.pallas_call(
        late_kernel,
        out_shape=(
            jax.ShapeDtypeStruct((span, D_LAT), jnp.bfloat16),
            jax.ShapeDtypeStruct((REQ, D_LAT), jnp.bfloat16),
        ),
        in_specs=[vmem] * 7,
        out_specs=(pl.BlockSpec(memory_space=pl.ANY), vmem),
        scratch_shapes=[
            keys,
            pltpu.VMEM((span, D_LAT), jnp.bfloat16),
            pltpu.SemaphoreType.DMA((n // 8,)),
        ],
        compiler_params=params,
        cost_estimate=cost,
        name="prefill_late",
    )(query_most, query_rest, received, received_swap, mixed, stats, moved)
    return prefill_out.reshape(span, 1, D_LAT), decode_out.reshape(REQ, 1, D_LAT)


def solution(mesh):
    n = mesh.shape["ctx"]
    in_specs = (
        P("groups", "ctx", None),
        P(("groups", "ctx"), None),
        P("groups", None, None),
        P("groups", "ctx", None),
        P("groups"),
        P("groups", None),
    )
    out_specs = (P("groups", "ctx", None), P("groups", "ctx", None))

    def body(*args):
        return shards(n, *args)

    return jax.shard_map(
        body, mesh=mesh, in_specs=in_specs, out_specs=out_specs, check_vma=False
    )
```

```python
import functools

import jax
import jax.numpy as jnp
from jax import lax
from jax.experimental import pallas as pl
from jax.experimental.pallas import tpu as pltpu
from jax.sharding import PartitionSpec as P

D_LAT = 512
PAGE = 16
POOL = 16
REQ = 2
LANES = 128

SCALE = 192.0 ** (-0.5)
LOG2E = 1.4426950408889634
NEG = -1e30

VMEM_LIMIT = 8 << 20
VMEM_MOST = 60 << 20


def bit_orders(n):
    bits = list(range(n.bit_length() - 2, 0, -1))
    return bits, bits[:-2] + bits[:-3:-1]


def permute_bits(rows, n, even_bit, odd_bit):
    pairs = [(i, i ^ (1 << (odd_bit if i & 1 else even_bit))) for i in range(n)]
    return lax.ppermute(rows, "ctx", pairs)


def decode_kernel(
    table_hbm,
    lengths_hbm,
    query_hbm,
    cache_hbm,
    latent_hbm,
    packed_ref,
    table_ref,
    lengths_ref,
    query_ref,
    cache_ref,
    latent_ref,
    sems,
):
    moves = [
        (cache_hbm.at[0], cache_ref.at[0]),
        (query_hbm, query_ref),
        (latent_hbm, latent_ref),
        (table_hbm, table_ref),
        (lengths_hbm, lengths_ref),
    ] + [(cache_hbm.at[r], cache_ref.at[r]) for r in range(1, REQ)]
    copies = [pltpu.make_async_copy(*move, sems.at[i]) for i, move in enumerate(moves)]
    for copy in copies:
        copy.start()

    device = lax.axis_index("ctx")
    rows = latent_ref.shape[0]
    length = cache_ref.shape[2]
    heads = query_ref.shape[1]
    first_page = (device * rows) // PAGE
    token = lax.broadcasted_iota(jnp.int32, (1, rows), 1)
    position = device * length + lax.broadcasted_iota(jnp.int32, (1, length), 1)
    lane = lax.broadcasted_iota(jnp.int32, (heads, LANES), 1)
    for copy in copies[1:5]:
        copy.wait()
    request = jnp.zeros((1, rows), jnp.int32)
    for k in range(max(1, rows // PAGE)):
        owner = table_ref[0, first_page + k]
        slot = table_ref[1, first_page + k]
        request = jnp.where(token // PAGE == k, lax.rem(owner * POOL + slot, REQ), request)
    latent = latent_ref[...]
    for r in range(REQ):
        query = query_ref[r]
        live = position < lengths_ref[r]
        mine = request == r
        page_scores = (
            lax.dot_general(
                query, latent, (((1,), (1,)), ((), ())), preferred_element_type=jnp.float32
            )
            * SCALE
        )
        copies[0 if r == 0 else 4 + r].wait()
        cache = cache_ref[r]
        cache_scores = jnp.dot(query, cache, preferred_element_type=jnp.float32) * SCALE
        top = jnp.maximum(
            jnp.max(jnp.where(live, cache_scores, NEG), axis=1, keepdims=True),
            jnp.max(jnp.where(mine, page_scores, NEG), axis=1, keepdims=True),
        )
        cache_weights = jnp.where(live, jnp.exp(cache_scores - top), 0.0)
        page_weights = jnp.where(mine, jnp.exp(page_scores - top), 0.0)
        total = jnp.sum(cache_weights, axis=1, keepdims=True) + jnp.sum(
            page_weights, axis=1, keepdims=True
        )
        mixed = lax.dot_general(
            cache_weights.astype(jnp.bfloat16),
            cache[:D_LAT],
            (((1,), (1,)), ((), ())),
            preferred_element_type=jnp.float32,
        ) + jnp.dot(
            page_weights.astype(jnp.bfloat16),
            latent[:, :D_LAT],
            preferred_element_type=jnp.float32,
        )
        packed_ref[:, r, :D_LAT] = mixed
        packed_ref[:, r, D_LAT:] = jnp.where(lane == 0, top, total)


def merge_kernel(moved_ref, decode_ref):
    moved = moved_ref[...]
    tops = moved[:, :, D_LAT : D_LAT + 1]
    totals = moved[:, :, D_LAT + 1 : D_LAT + 2]
    scales = jnp.exp(tops - jnp.max(tops, axis=0, keepdims=True))
    own_out = jnp.sum(moved[:, :, :D_LAT] * scales, axis=0)
    decode_ref[...] = (own_out / jnp.sum(totals * scales, axis=0)).astype(jnp.bfloat16)


def turn_kernel(start, turned_ref, query_ref):
    query_ref[...] = turned_ref[:, start : start + query_ref.shape[0]].T


def turn_query(turned, start, count, params):
    width = turned.shape[0]
    vmem = pl.BlockSpec(memory_space=pltpu.VMEM)
    return pl.pallas_call(
        functools.partial(turn_kernel, start),
        out_shape=jax.ShapeDtypeStruct((count, width), jnp.bfloat16),
        in_specs=[vmem],
        out_specs=vmem,
        compiler_params=params,
        cost_estimate=pl.CostEstimate(
            flops=0, bytes_accessed=4 * count * width, transcendentals=0
        ),
        name="turn_query",
    )(turned)


def place_keys(own_ref, swap_ref, keys, late):
    device = lax.axis_index("ctx")
    parity = lax.rem(device, 2)
    slots, rows, _ = own_ref.shape
    groups = slots // 2
    bits = (groups * 8).bit_length() - 1
    offsets = []
    for side, ref in enumerate((own_ref, swap_ref)):
        odd = parity ^ side
        third = jnp.where(odd == 1, 2, 4)
        fourth = 6 - third
        base = (device & 7) ^ side
        if late:
            base = base ^ fourth
        for half in range(2):
            offsets.append((base ^ third) if half else base)
            place = 2 * side + half
            for t in range(groups):
                mask = 0
                for step in range(bits - 3):
                    if (t >> step) & 1:
                        mask |= 1 << (bits - 4 - step)
                group = (device // 8) ^ mask
                start = pl.multiple_of((group * 4 + place) * rows, rows)
                keys[pl.ds(start, rows)] = ref[half * groups + t]
    column = lax.broadcasted_iota(jnp.int32, (1, 4 * rows), 1)
    token = jnp.zeros((1, 4 * rows), jnp.int32)
    for place, low in enumerate(offsets):
        token = jnp.where(column // rows == place, low * rows + lax.rem(column, rows), token)
    return token


def block_scores(query, keys, token, index, block, columns):
    scores = lax.dot_general(
        query,
        keys[: (index + 1) * columns],
        (((1,), (1,)), ((), ())),
        preferred_element_type=jnp.float32,
    )
    row = lax.broadcasted_iota(jnp.int32, (block, columns), 0)
    diagonal = jnp.where(token <= row, scores[:, index * columns :], NEG)
    if index == 0:
        return diagonal
    return jnp.concatenate([scores[:, : index * columns], diagonal], axis=1)


def early_kernel(
    most_ref, rest_ref, own_ref, swap_ref, mixed_hbm, stats_ref, keys, mixed_ref, sems
):
    token = place_keys(own_ref, swap_ref, keys, False)
    columns = token.shape[1]
    block = 2 * columns
    lane = lax.broadcasted_iota(jnp.int32, (block, LANES), 1)
    last = most_ref.shape[0] // block
    copies = []
    for index in range(last, -1, -1):
        span = pl.ds(index * block, block)
        query = rest_ref[...] if index == last else most_ref[span]
        scores = block_scores(query, keys, token, index, block, columns)
        top = jnp.max(scores, axis=1, keepdims=True)
        weights = jnp.exp2((scores - top) * (SCALE * LOG2E))
        total = jnp.sum(weights, axis=1, keepdims=True)
        mixed_ref[span] = jnp.dot(
            weights.astype(jnp.bfloat16),
            keys[: (index + 1) * columns, :D_LAT],
            preferred_element_type=jnp.float32,
        )
        stats_ref[span] = jnp.where(lane == 0, top, total)
        copy = pltpu.make_async_copy(mixed_ref.at[span], mixed_hbm.at[span], sems.at[index])
        copy.start()
        copies.append(copy)
    for copy in copies:
        copy.wait()


def late_kernel(
    most_ref,
    rest_ref,
    own_ref,
    swap_ref,
    mixed_hbm,
    stats_ref,
    out_ref,
    keys,
    mixed_ref,
    blocks,
    in_sems,
    out_sems,
):
    columns = 4 * own_ref.shape[1]
    block = 2 * columns
    last = most_ref.shape[0] // block
    spans = [pl.ds(index * block, block) for index in range(last + 1)]
    loads = [
        pltpu.make_async_copy(mixed_hbm.at[span], mixed_ref.at[span], in_sems.at[index])
        for index, span in enumerate(spans)
    ]
    for load in loads[::-1]:
        load.start()
    token = place_keys(own_ref, swap_ref, keys, True)
    stores = []
    for index in range(last, -1, -1):
        span = spans[index]
        query = rest_ref[...] if index == last else most_ref[span]
        scores = block_scores(query, keys, token, index, block, columns)
        before = stats_ref[span, 0:1]
        top = jnp.maximum(jnp.max(scores, axis=1, keepdims=True), before)
        weights = jnp.exp2((scores - top) * (SCALE * LOG2E))
        factor = jnp.exp2((before - top) * (SCALE * LOG2E))
        total = jnp.sum(weights, axis=1, keepdims=True) + stats_ref[span, 1:2] * factor
        mixed = jnp.dot(
            weights.astype(jnp.bfloat16),
            keys[: (index + 1) * columns, :D_LAT],
            preferred_element_type=jnp.float32,
        )
        scale = 1.0 / total
        loads[index].wait()
        blocks[span] = (mixed_ref[span] * (factor * scale) + mixed * scale).astype(jnp.bfloat16)
        store = pltpu.make_async_copy(blocks.at[span], out_ref.at[span], out_sems.at[index])
        store.start()
        stores.append(store)
    for store in stores:
        store.wait()


def shards(n, prefill_query, prefill_latent, decode_query, cache, lengths, page_table):
    span = prefill_query.shape[0]
    rows, width = prefill_latent.shape
    heads = decode_query.shape[1]
    vmem = pl.BlockSpec(memory_space=pltpu.VMEM)
    hbm = pl.BlockSpec(memory_space=pltpu.HBM)
    params = pltpu.CompilerParams(vmem_limit_bytes=VMEM_LIMIT)

    even_bits, odd_bits = bit_orders(n)
    held = prefill_latent[None]
    for step, (even, odd) in enumerate(zip(even_bits, odd_bits)):
        received = permute_bits(held, n, even, odd)
        if step < len(even_bits) - 1:
            held = jnp.concatenate([held, received], axis=0)
    held_swap = permute_bits(held, n, 0, 0)
    received_swap = permute_bits(received, n, 0, 0)

    packed = pl.pallas_call(
        decode_kernel,
        out_shape=jax.ShapeDtypeStruct((heads, REQ, D_LAT + LANES), jnp.float32),
        in_specs=[hbm] * 5,
        out_specs=vmem,
        scratch_shapes=[
            pltpu.SMEM(page_table.shape[::-1], jnp.int32),
            pltpu.SMEM(lengths.shape, jnp.int32),
            pltpu.VMEM(decode_query.shape, jnp.bfloat16),
            pltpu.VMEM((REQ, width, cache.shape[1]), jnp.bfloat16),
            pltpu.VMEM((rows, width), jnp.bfloat16),
            pltpu.SemaphoreType.DMA((4 + REQ,)),
        ],
        compiler_params=pltpu.CompilerParams(vmem_limit_bytes=VMEM_MOST),
        cost_estimate=pl.CostEstimate(
            flops=4 * cache.size * heads, bytes_accessed=2 * cache.size, transcendentals=0
        ),
        name="decode_part",
    )(page_table.T, lengths, decode_query, jnp.swapaxes(cache, 1, 2), prefill_latent)
    moved = lax.all_to_all(packed, "ctx", split_axis=0, concat_axis=0, tiled=True)

    turned = jnp.transpose(prefill_query, (1, 2, 0)).reshape(width, span)
    block = 8 * rows
    query_most = turn_query(turned, 0, span - block, params)
    query_rest = turn_query(turned, span - block, block, params)

    cost = pl.CostEstimate(
        flops=2 * span * span * width, bytes_accessed=4 * span * width, transcendentals=0
    )
    keys = pltpu.VMEM((span // 2, width), jnp.bfloat16)
    sums = pltpu.VMEM((span, D_LAT), jnp.float32)
    sems = pltpu.SemaphoreType.DMA((n // 8,))
    mixed, stats = pl.pallas_call(
        early_kernel,
        out_shape=(
            pltpu.HBM((span, D_LAT), jnp.float32),
            jax.ShapeDtypeStruct((span, LANES), jnp.float32),
        ),
        in_specs=[vmem] * 4,
        out_specs=(hbm, vmem),
        scratch_shapes=[keys, sums, sems],
        compiler_params=params,
        cost_estimate=cost,
        name="prefill_early",
    )(query_most, query_rest, held, held_swap)
    decode_out = pl.pallas_call(
        merge_kernel,
        out_shape=jax.ShapeDtypeStruct((REQ, D_LAT), jnp.bfloat16),
        in_specs=[vmem],
        out_specs=vmem,
        compiler_params=params,
        cost_estimate=pl.CostEstimate(flops=moved.size, bytes_accessed=16, transcendentals=0),
        name="decode_merge",
    )(moved)
    prefill_out = pl.pallas_call(
        late_kernel,
        out_shape=jax.ShapeDtypeStruct((span, D_LAT), jnp.bfloat16),
        in_specs=[vmem] * 4 + [hbm, vmem],
        out_specs=hbm,
        scratch_shapes=[keys, sums, pltpu.VMEM((span, D_LAT), jnp.bfloat16), sems, sems],
        compiler_params=params,
        cost_estimate=cost,
        name="prefill_late",
    )(query_most, query_rest, received, received_swap, mixed, stats)
    return prefill_out.reshape(span, 1, D_LAT), decode_out.reshape(REQ, 1, D_LAT)


def solution(mesh):
    n = mesh.shape["ctx"]
    in_specs = (
        P("groups", "ctx", None),
        P(("groups", "ctx"), None),
        P("groups", None, None),
        P("groups", "ctx", None),
        P("groups"),
        P("groups", None),
    )
    out_specs = (P("groups", "ctx", None), P("groups", "ctx", None))

    def body(*args):
        return shards(n, *args)

    return jax.shard_map(
        body, mesh=mesh, in_specs=in_specs, out_specs=out_specs, check_vma=False
    )
```

```python
import functools

import jax
import jax.numpy as jnp
from jax import lax
from jax.experimental import pallas as pl
from jax.experimental.pallas import tpu as pltpu
from jax.sharding import PartitionSpec as P

D_LAT = 512
PAGE = 16
POOL = 16
REQ = 2
LANES = 128
GROUP = D_LAT // LANES

SCALE = 192.0 ** (-0.5)
LOG2E = 1.4426950408889634
NEG = -1e30
SOFTMAX_ROWS = 64

VMEM_LIMIT = 8 << 20
VMEM_MOST = 60 << 20


def bit_orders(n):
    bits = list(range(n.bit_length() - 2, 0, -1))
    return bits, bits[-1:] + bits[:-1]


def permute_bits(rows, n, even_bit, odd_bit):
    pairs = [(i, i ^ (1 << (odd_bit if i & 1 else even_bit))) for i in range(n)]
    return lax.ppermute(rows, "ctx", pairs)


def split_parts(value):
    parts = []
    for _ in range(3):
        part = value.astype(jnp.bfloat16).astype(jnp.float32)
        parts.append(part)
        value = value - part
    return parts


def pack_stats(top, total, lane):
    stats = jnp.zeros((top.shape[0], LANES), jnp.float32)
    for k, part in enumerate(split_parts(top) + split_parts(total)):
        stats = jnp.where(lane == k, part, stats)
    return stats


def spread_stats(packed):
    source = lax.broadcasted_iota(jnp.int32, (LANES, 2 * LANES), 0)
    target = lax.broadcasted_iota(jnp.int32, (LANES, 2 * LANES), 1)
    ones = jnp.where(source // 3 == target // LANES, 1.0, 0.0).astype(jnp.bfloat16)
    return jnp.dot(packed, ones, preferred_element_type=jnp.float32)


def decode_kernel(
    table_hbm,
    lengths_hbm,
    query_hbm,
    cache_hbm,
    latent_hbm,
    packed_ref,
    table_ref,
    lengths_ref,
    query_ref,
    cache_ref,
    latent_ref,
    rows_ref,
    sems,
):
    moves = [
        (cache_hbm.at[0], cache_ref.at[0]),
        (query_hbm, query_ref),
        (latent_hbm, latent_ref),
        (table_hbm, table_ref),
        (lengths_hbm, lengths_ref),
    ] + [(cache_hbm.at[r], cache_ref.at[r]) for r in range(1, REQ)]
    copies = [pltpu.make_async_copy(*move, sems.at[i]) for i, move in enumerate(moves)]
    for copy in copies:
        copy.start()

    device = lax.axis_index("ctx")
    rows = latent_ref.shape[0]
    length = cache_ref.shape[2]
    heads = query_ref.shape[1]
    first_page = (device * rows) // PAGE
    token = lax.broadcasted_iota(jnp.int32, (1, rows), 1)
    position = device * length + lax.broadcasted_iota(jnp.int32, (1, length), 1)
    lane = lax.broadcasted_iota(jnp.int32, (heads, LANES), 1)
    for copy in copies[1:5]:
        copy.wait()
    request = jnp.zeros((1, rows), jnp.int32)
    for k in range(max(1, rows // PAGE)):
        owner = table_ref[0, first_page + k]
        slot = table_ref[1, first_page + k]
        request = jnp.where(token // PAGE == k, lax.rem(owner * POOL + slot, REQ), request)
    latent = latent_ref[...]
    for r in range(REQ):
        query = query_ref[r]
        live = position < lengths_ref[r]
        mine = request == r
        page_scores = (
            lax.dot_general(
                query, latent, (((1,), (1,)), ((), ())), preferred_element_type=jnp.float32
            )
            * SCALE
        )
        copies[0 if r == 0 else 4 + r].wait()
        cache = cache_ref[r]
        cache_scores = jnp.dot(query, cache, preferred_element_type=jnp.float32) * SCALE
        top = jnp.maximum(
            jnp.max(jnp.where(live, cache_scores, NEG), axis=1, keepdims=True),
            jnp.max(jnp.where(mine, page_scores, NEG), axis=1, keepdims=True),
        )
        cache_weights = jnp.where(live, jnp.exp(cache_scores - top), 0.0)
        page_weights = jnp.where(mine, jnp.exp(page_scores - top), 0.0)
        total = jnp.sum(cache_weights, axis=1, keepdims=True) + jnp.sum(
            page_weights, axis=1, keepdims=True
        )
        mixed = lax.dot_general(
            cache_weights.astype(jnp.bfloat16),
            cache[:D_LAT],
            (((1,), (1,)), ((), ())),
            preferred_element_type=jnp.float32,
        ) + jnp.dot(
            page_weights.astype(jnp.bfloat16),
            latent[:, :D_LAT],
            preferred_element_type=jnp.float32,
        )
        stats = pack_stats(top, total, lane)
        for j in range(GROUP):
            rows_ref[:, GROUP * r + j] = mixed[:, LANES * j : LANES * (j + 1)]
            rows_ref[:, GROUP * (REQ + r) + j] = stats
    packed_ref[...] = rows_ref[...].astype(jnp.bfloat16)


def merge_kernel(moved_ref, decode_ref):
    half = REQ * GROUP
    moved = moved_ref[...]
    stats = spread_stats(moved.reshape(-1, LANES))
    stats = stats.reshape(moved.shape[0], 2 * half, 2 * LANES)[:, half:]
    tops = stats[:, :, :LANES]
    scales = jnp.exp(tops - jnp.max(tops, axis=0, keepdims=True))
    mixed = jnp.sum(moved.astype(jnp.float32)[:, :half] * scales, axis=0)
    merged = (mixed / jnp.sum(stats[:, :, LANES:] * scales, axis=0)).astype(jnp.bfloat16)
    for r in range(REQ):
        for j in range(GROUP):
            row = GROUP * r + j
            decode_ref[r : r + 1, LANES * j : LANES * (j + 1)] = merged[row : row + 1]


def join_kernel(held_ref, received_ref, joined_ref):
    count = held_ref.shape[0]
    joined_ref[:count] = held_ref[...]
    joined_ref[count:] = received_ref[...]


def join_slots(held, received, params):
    vmem = pl.BlockSpec(memory_space=pltpu.VMEM)
    shape = (held.shape[0] + received.shape[0], *held.shape[1:])
    return pl.pallas_call(
        join_kernel,
        out_shape=jax.ShapeDtypeStruct(shape, held.dtype),
        in_specs=[vmem, vmem],
        out_specs=vmem,
        compiler_params=params,
        cost_estimate=pl.CostEstimate(flops=0, bytes_accessed=4 * held.size, transcendentals=0),
        name="join_slots",
    )(held, received)


def turn_kernel(turned_ref, query_ref):
    query_ref[...] = turned_ref[...].T


def placed_tokens(shape, rows):
    device = lax.axis_index("ctx")
    column = lax.broadcasted_iota(jnp.int32, shape, 1)
    place = lax.rem(column // rows, 4)
    low = jnp.zeros_like(column)
    for number in range(4):
        side = number // 2
        third = jnp.where((device & 1) ^ side == 1, 2, 4)
        base = (device & 7) ^ side
        low = jnp.where(place == number, base ^ third if number % 2 else base, low)
    return ((column // (rows * 4)) * 8 + low) * rows + lax.rem(column, rows)


def slot_tokens(shape, rows, slots, side):
    device = lax.axis_index("ctx")
    groups = slots // 2
    third = jnp.where((device & 1) ^ side == 1, 2, 4)
    column = lax.broadcasted_iota(jnp.int32, shape, 1)
    slot = column // rows
    odd = third == 2
    half = jnp.where(odd, slot & 1, slot // groups)
    high = jnp.where(odd, slot >> 1, slot & (groups - 1))
    owner = (device ^ side ^ (6 - third)) ^ (half * third)
    bits = groups.bit_length() - 1
    for step in range(bits):
        owner = owner ^ (((high >> step) & 1) * (8 << (bits - 1 - step)))
    return owner * rows + lax.rem(column, rows)


def tokens_kernel(n, rows, tokens_ref):
    shape = (1, tokens_ref.shape[1])
    tokens_ref[0:1] = placed_tokens(shape, rows)
    for side in range(2):
        tokens_ref[1 + side : 2 + side] = slot_tokens(shape, rows, n // 4, side)


def place_keys(refs, keys):
    device = lax.axis_index("ctx")
    slots, rows, _ = refs[0].shape
    groups = slots // 2
    bits = groups.bit_length() - 1

    def mask(high):
        return sum(8 << (bits - 1 - step) for step in range(bits) if (high >> step) & 1) // 8

    for side, ref in enumerate(refs):
        odd = (device & 1) ^ side == 1
        for t in range(slots):
            group = (device // 8) ^ jnp.where(odd, mask(t >> 1), mask(t & (groups - 1)))
            place = 2 * side + jnp.where(odd, t & 1, t // groups)
            keys[pl.ds(pl.multiple_of((group * 4 + place) * rows, rows), rows)] = ref[t]


def spread(column):
    return jnp.broadcast_to(column, (column.shape[0], LANES))


def block_weights(query, keys, token, first):
    scores = lax.dot_general(
        query, keys, (((1,), (1,)), ((), ())), preferred_element_type=jnp.float32
    )
    block, count = scores.shape
    row = first + lax.broadcasted_iota(jnp.int32, (block, count), 0)
    scores = jnp.where(token <= row, scores, NEG)
    top = jnp.max(scores, axis=1, keepdims=True)
    weights = jnp.exp2((scores - top) * (SCALE * LOG2E))
    total = jnp.sum(weights, axis=1, keepdims=True)
    mixed = jnp.dot(
        weights.astype(jnp.bfloat16), keys[:, :D_LAT], preferred_element_type=jnp.float32
    )
    return top, total, mixed


def early_kernel(tokens_ref, query_ref, own_ref, swap_ref, mixed_ref, keys):
    place_keys((own_ref, swap_ref), keys)
    lane = lax.broadcasted_iota(jnp.int32, (1, LANES), 1)
    block = 8 * own_ref.shape[1]
    count = query_ref.shape[0] // block
    columns = keys.shape[0] // count
    for index in range(count - 1, -1, -1):
        rows = slice(index * block, (index + 1) * block)
        upto = (index + 1) * columns
        top, total, mixed = block_weights(
            query_ref[rows], keys[:upto], tokens_ref[0:1, :upto], index * block
        )
        mixed_ref[rows, :D_LAT] = mixed.astype(jnp.bfloat16)
        mixed_ref[rows, D_LAT:] = pack_stats(top, total, lane).astype(jnp.bfloat16)


def fold_keys(query_ref, keys, token, stats_of, scores, weights):
    cut = scores.shape[0] * 3 // 4
    for part in (slice(cut, None), slice(0, cut)):
        scores[part] = lax.dot_general(
            query_ref[part], keys, (((1,), (1,)), ((), ())), preferred_element_type=jnp.float32
        )
    span, count = scores.shape
    block = min(SOFTMAX_ROWS, span)
    for first in range(0, span, block):
        rows = slice(first, first + block)
        row = first + lax.broadcasted_iota(jnp.int32, (block, count), 0)
        masked = jnp.where(token <= row, scores[rows], NEG)
        before, former = stats_of(rows)
        top = jnp.maximum(spread(jnp.max(masked, axis=1, keepdims=True)), before)
        total = jnp.zeros_like(top)
        for c in range(0, count, LANES):
            part = jnp.exp2((masked[:, c : c + LANES] - top) * (SCALE * LOG2E))
            weights[rows, c : c + LANES] = part.astype(jnp.bfloat16)
            total = total + part
        total = spread(jnp.sum(total, axis=1, keepdims=True))
        factor = jnp.exp2((before - top) * (SCALE * LOG2E))
        yield rows, top, factor, former * factor + total


def middle_kernel(
    tokens_ref,
    query_ref,
    own_ref,
    former_ref,
    mixed_ref,
    top_ref,
    total_ref,
    scores,
    weights,
    factors,
    stats,
):
    stats[...] = spread_stats(former_ref[:, D_LAT:])

    def stats_of(rows):
        return stats[rows, :LANES], stats[rows, LANES:]

    keys = own_ref[...].reshape(-1, own_ref.shape[2])
    token = tokens_ref[1:2, : keys.shape[0]]
    for rows, top, factor, total in fold_keys(query_ref, keys, token, stats_of, scores, weights):
        top_ref[rows] = top
        total_ref[rows] = total
        factors[rows] = factor
    values = keys[:, :D_LAT]
    block = 8 * own_ref.shape[1]
    for first in range(0, scores.shape[0], block):
        rows = slice(first, first + block)
        mixed = jnp.dot(weights[rows], values, preferred_element_type=jnp.float32)
        for c in range(0, D_LAT, LANES):
            part = slice(c, c + LANES)
            mixed_ref[rows, part] = (
                former_ref[rows, part].astype(jnp.float32) * factors[rows] + mixed[:, part]
            )


def late_kernel(
    tokens_ref,
    query_ref,
    swap_ref,
    former_ref,
    top_ref,
    total_ref,
    merged_ref,
    out_ref,
    decode_ref,
    scores,
    weights,
    factors,
    scales,
    blocks,
    sems,
):
    stores = [pltpu.make_async_copy(merged_ref, decode_ref, sems.at[0])]
    stores[0].start()

    def stats_of(rows):
        return top_ref[rows], total_ref[rows]

    keys = swap_ref[...].reshape(-1, swap_ref.shape[2])
    token = tokens_ref[2:3, : keys.shape[0]]
    for rows, _, factor, total in fold_keys(query_ref, keys, token, stats_of, scores, weights):
        scale = 1.0 / total
        scales[rows] = scale
        factors[rows] = factor * scale
    values = keys[:, :D_LAT]
    block = 8 * swap_ref.shape[1]
    for first in range(0, scores.shape[0], block):
        rows = slice(first, first + block)
        mixed = jnp.dot(weights[rows], values, preferred_element_type=jnp.float32)
        for c in range(0, D_LAT, LANES):
            part = slice(c, c + LANES)
            blocks[rows, part] = (
                former_ref[rows, part] * factors[rows] + mixed[:, part] * scales[rows]
            ).astype(jnp.bfloat16)
        span = pl.ds(first, block)
        store = pltpu.make_async_copy(blocks.at[span], out_ref.at[span], sems.at[len(stores)])
        store.start()
        stores.append(store)
    for store in stores:
        store.wait()


def shards(n, prefill_query, prefill_latent, decode_query, cache, lengths, page_table):
    span = prefill_query.shape[0]
    rows, width = prefill_latent.shape
    heads = decode_query.shape[1]
    vmem = pl.BlockSpec(memory_space=pltpu.VMEM)
    hbm = pl.BlockSpec(memory_space=pltpu.HBM)
    params = pltpu.CompilerParams(vmem_limit_bytes=VMEM_LIMIT)

    packed = pl.pallas_call(
        decode_kernel,
        out_shape=jax.ShapeDtypeStruct((heads, 2 * REQ * GROUP, LANES), jnp.bfloat16),
        in_specs=[hbm] * 5,
        out_specs=vmem,
        scratch_shapes=[
            pltpu.SMEM(page_table.shape[::-1], jnp.int32),
            pltpu.SMEM(lengths.shape, jnp.int32),
            pltpu.VMEM(decode_query.shape, jnp.bfloat16),
            pltpu.VMEM((REQ, width, cache.shape[1]), jnp.bfloat16),
            pltpu.VMEM((rows, width), jnp.bfloat16),
            pltpu.VMEM((heads, 2 * REQ * GROUP, LANES), jnp.float32),
            pltpu.SemaphoreType.DMA((4 + REQ,)),
        ],
        compiler_params=pltpu.CompilerParams(vmem_limit_bytes=VMEM_MOST),
        cost_estimate=pl.CostEstimate(
            flops=4 * cache.size * heads, bytes_accessed=2 * cache.size, transcendentals=0
        ),
        name="decode_part",
    )(page_table.T, lengths, decode_query, jnp.swapaxes(cache, 1, 2), prefill_latent)
    even_bits, odd_bits = bit_orders(n)
    held = prefill_latent[None]
    for step, (even, odd) in enumerate(zip(even_bits, odd_bits)):
        received = permute_bits(held, n, even, odd)
        if step < len(even_bits) - 1:
            held = join_slots(held, received, params)
    held_swap = permute_bits(held, n, 0, 0)
    received_swap = permute_bits(received, n, 0, 0)

    moved = lax.all_to_all(packed, "ctx", split_axis=0, concat_axis=0, tiled=True)

    query = pl.pallas_call(
        turn_kernel,
        out_shape=jax.ShapeDtypeStruct((span, width), jnp.bfloat16),
        in_specs=[vmem],
        out_specs=vmem,
        compiler_params=params,
        cost_estimate=pl.CostEstimate(flops=0, bytes_accessed=4 * span * width, transcendentals=0),
        name="turn_query",
    )(jnp.transpose(prefill_query, (1, 2, 0)).reshape(width, span))
    tokens = pl.pallas_call(
        functools.partial(tokens_kernel, n, rows),
        out_shape=jax.ShapeDtypeStruct((3, span // 2), jnp.int32),
        in_specs=[],
        out_specs=vmem,
        compiler_params=params,
        cost_estimate=pl.CostEstimate(flops=span, bytes_accessed=16, transcendentals=0),
        name="key_tokens",
    )()

    def cost(share):
        return pl.CostEstimate(
            flops=4 * span * span * width // share,
            bytes_accessed=4 * span * width,
            transcendentals=0,
        )

    sums = jax.ShapeDtypeStruct((span, D_LAT), jnp.float32)
    stat = jax.ShapeDtypeStruct((span, LANES), jnp.float32)
    quarter = span // 4
    scratch = [
        pltpu.VMEM((span, quarter), jnp.float32),
        pltpu.VMEM((span, quarter), jnp.bfloat16),
        pltpu.VMEM((span, LANES), jnp.float32),
    ]
    early = pl.pallas_call(
        early_kernel,
        out_shape=jax.ShapeDtypeStruct((span, D_LAT + LANES), jnp.bfloat16),
        in_specs=[vmem] * 4,
        out_specs=vmem,
        scratch_shapes=[pltpu.VMEM((span // 2, width), jnp.bfloat16)],
        compiler_params=params,
        cost_estimate=cost(2),
        name="prefill_early",
    )(tokens, query, held, held_swap)
    merged = pl.pallas_call(
        merge_kernel,
        out_shape=jax.ShapeDtypeStruct((REQ, D_LAT), jnp.bfloat16),
        in_specs=[vmem],
        out_specs=vmem,
        compiler_params=params,
        cost_estimate=pl.CostEstimate(flops=moved.size, bytes_accessed=16, transcendentals=0),
        name="decode_merge",
    )(moved)
    mixed, top, total = pl.pallas_call(
        middle_kernel,
        out_shape=(sums, stat, stat),
        in_specs=[vmem] * 4,
        out_specs=(vmem, vmem, vmem),
        scratch_shapes=scratch + [pltpu.VMEM((span, 2 * LANES), jnp.float32)],
        compiler_params=params,
        cost_estimate=cost(4),
        name="prefill_middle",
    )(tokens, query, received, early)
    prefill_out, decode_out = pl.pallas_call(
        late_kernel,
        out_shape=(
            jax.ShapeDtypeStruct((span, D_LAT), jnp.bfloat16),
            jax.ShapeDtypeStruct((REQ, D_LAT), jnp.bfloat16),
        ),
        in_specs=[vmem] * 7,
        out_specs=(hbm, hbm),
        scratch_shapes=scratch
        + [
            pltpu.VMEM((span, LANES), jnp.float32),
            pltpu.VMEM((span, D_LAT), jnp.bfloat16),
            pltpu.SemaphoreType.DMA((1 + n // 8,)),
        ],
        compiler_params=params,
        cost_estimate=cost(4),
        name="prefill_late",
    )(tokens, query, received_swap, mixed, top, total, merged)
    return prefill_out.reshape(span, 1, D_LAT), decode_out.reshape(REQ, 1, D_LAT)


def solution(mesh):
    n = mesh.shape["ctx"]
    in_specs = (
        P("groups", "ctx", None),
        P(("groups", "ctx"), None),
        P("groups", None, None),
        P("groups", "ctx", None),
        P("groups"),
        P("groups", None),
    )
    out_specs = (P("groups", "ctx", None), P("groups", "ctx", None))

    def body(*args):
        return shards(n, *args)

    return jax.shard_map(
        body, mesh=mesh, in_specs=in_specs, out_specs=out_specs, check_vma=False
    )
```

```python
import functools

import jax
import jax.numpy as jnp
from jax import lax
from jax.experimental import pallas as pl
from jax.experimental.pallas import tpu as pltpu
from jax.sharding import PartitionSpec as P

D_LAT = 512
PAGE = 16
POOL = 16
REQ = 2
LANES = 128
GROUP = D_LAT // LANES

SCALE = 192.0 ** (-0.5)
LOG2E = 1.4426950408889634
NEG = -1e30
SOFTMAX_ROWS = 64

VMEM_LIMIT = 12 << 20
VMEM_MOST = 60 << 20


def permute_mask(rows, n, mask):
    return lax.ppermute(rows, "ctx", [(i, i ^ mask) for i in range(n)])


def split_parts(value):
    parts = []
    for _ in range(3):
        part = value.astype(jnp.bfloat16).astype(jnp.float32)
        parts.append(part)
        value = value - part
    return parts


def pack_stats(top, total, lane):
    stats = jnp.zeros((top.shape[0], LANES), jnp.float32)
    for k, part in enumerate(split_parts(top) + split_parts(total)):
        stats = jnp.where(lane == k, part, stats)
    return stats


def spread_stats(packed):
    source = lax.broadcasted_iota(jnp.int32, (LANES, 2 * LANES), 0)
    target = lax.broadcasted_iota(jnp.int32, (LANES, 2 * LANES), 1)
    ones = jnp.where(source // 3 == target // LANES, 1.0, 0.0).astype(jnp.bfloat16)
    return jnp.dot(packed, ones, preferred_element_type=jnp.float32)


def decode_kernel(
    table_hbm,
    lengths_hbm,
    query_hbm,
    cache_hbm,
    latent_hbm,
    packed_ref,
    table_ref,
    lengths_ref,
    query_ref,
    cache_ref,
    latent_ref,
    rows_ref,
    sems,
):
    moves = [
        (cache_hbm.at[0], cache_ref.at[0]),
        (query_hbm, query_ref),
        (latent_hbm, latent_ref),
        (table_hbm, table_ref),
        (lengths_hbm, lengths_ref),
    ] + [(cache_hbm.at[r], cache_ref.at[r]) for r in range(1, REQ)]
    copies = [pltpu.make_async_copy(*move, sems.at[i]) for i, move in enumerate(moves)]
    for copy in copies:
        copy.start()

    device = lax.axis_index("ctx")
    rows = latent_ref.shape[0]
    length = cache_ref.shape[2]
    heads = query_ref.shape[1]
    first_page = (device * rows) // PAGE
    token = lax.broadcasted_iota(jnp.int32, (1, rows), 1)
    position = device * length + lax.broadcasted_iota(jnp.int32, (1, length), 1)
    lane = lax.broadcasted_iota(jnp.int32, (heads, LANES), 1)
    for copy in copies[1:5]:
        copy.wait()
    request = jnp.zeros((1, rows), jnp.int32)
    for k in range(max(1, rows // PAGE)):
        owner = table_ref[0, first_page + k]
        slot = table_ref[1, first_page + k]
        request = jnp.where(token // PAGE == k, lax.rem(owner * POOL + slot, REQ), request)
    latent = latent_ref[...]
    for r in range(REQ):
        query = query_ref[r]
        live = position < lengths_ref[r]
        mine = request == r
        page_scores = (
            lax.dot_general(
                query, latent, (((1,), (1,)), ((), ())), preferred_element_type=jnp.float32
            )
            * SCALE
        )
        copies[0 if r == 0 else 4 + r].wait()
        cache = cache_ref[r]
        cache_scores = jnp.dot(query, cache, preferred_element_type=jnp.float32) * SCALE
        top = jnp.maximum(
            jnp.max(jnp.where(live, cache_scores, NEG), axis=1, keepdims=True),
            jnp.max(jnp.where(mine, page_scores, NEG), axis=1, keepdims=True),
        )
        cache_weights = jnp.where(live, jnp.exp(cache_scores - top), 0.0)
        page_weights = jnp.where(mine, jnp.exp(page_scores - top), 0.0)
        total = jnp.sum(cache_weights, axis=1, keepdims=True) + jnp.sum(
            page_weights, axis=1, keepdims=True
        )
        mixed = lax.dot_general(
            cache_weights.astype(jnp.bfloat16),
            cache[:D_LAT],
            (((1,), (1,)), ((), ())),
            preferred_element_type=jnp.float32,
        ) + jnp.dot(
            page_weights.astype(jnp.bfloat16),
            latent[:, :D_LAT],
            preferred_element_type=jnp.float32,
        )
        stats = pack_stats(top, total, lane)
        for j in range(GROUP):
            rows_ref[:, GROUP * r + j] = mixed[:, LANES * j : LANES * (j + 1)]
            rows_ref[:, GROUP * (REQ + r) + j] = stats
    packed_ref[...] = rows_ref[...].astype(jnp.bfloat16)


def merge_kernel(moved_ref, decode_ref):
    half = REQ * GROUP
    moved = moved_ref[...]
    stats = spread_stats(moved.reshape(-1, LANES))
    stats = stats.reshape(moved.shape[0], 2 * half, 2 * LANES)[:, half:]
    tops = stats[:, :, :LANES]
    scales = jnp.exp(tops - jnp.max(tops, axis=0, keepdims=True))
    mixed = jnp.sum(moved.astype(jnp.float32)[:, :half] * scales, axis=0)
    merged = (mixed / jnp.sum(stats[:, :, LANES:] * scales, axis=0)).astype(jnp.bfloat16)
    for r in range(REQ):
        for j in range(GROUP):
            row = GROUP * r + j
            decode_ref[r : r + 1, LANES * j : LANES * (j + 1)] = merged[row : row + 1]


def join_kernel(held_ref, received_ref, joined_ref):
    count = held_ref.shape[0]
    joined_ref[:count] = held_ref[...]
    joined_ref[count:] = received_ref[...]


def join_slots(held, received, params):
    vmem = pl.BlockSpec(memory_space=pltpu.VMEM)
    shape = (held.shape[0] + received.shape[0], *held.shape[1:])
    return pl.pallas_call(
        join_kernel,
        out_shape=jax.ShapeDtypeStruct(shape, held.dtype),
        in_specs=[vmem, vmem],
        out_specs=vmem,
        compiler_params=params,
        cost_estimate=pl.CostEstimate(flops=0, bytes_accessed=4 * held.size, transcendentals=0),
        name="join_slots",
    )(held, received)


def turn_kernel(turned_ref, query_ref):
    query_ref[...] = turned_ref[...].T


def tokens_kernel(n, rows, tokens_ref):
    device = lax.axis_index("ctx")
    shape = (1, tokens_ref.shape[1])
    groups = n // 8
    column = lax.broadcasted_iota(jnp.int32, shape, 1)
    slot = column // rows
    group = jnp.full_like(column, device // 8)
    bits = groups.bit_length() - 1
    for step in range(bits):
        group = group ^ (((slot >> step) & 1) << (bits - 1 - step))
    number = slot // groups
    for kernel, low in enumerate((number, 2 * (number + 1), 2 * (number + 1) + 1)):
        owner = group * 8 + ((device & 7) ^ low)
        tokens_ref[kernel : kernel + 1] = owner * rows + lax.rem(column, rows)


def spread(column):
    return jnp.broadcast_to(column, (column.shape[0], LANES))


def joined_keys(refs):
    return jnp.concatenate([ref[...].reshape(-1, ref.shape[2]) for ref in refs], axis=0)


def fold_keys(query_ref, keys, token, stats_of, scores, weights):
    cut = scores.shape[0] * 3 // 4
    for part in (slice(cut, None), slice(0, cut)):
        scores[part] = lax.dot_general(
            query_ref[part], keys, (((1,), (1,)), ((), ())), preferred_element_type=jnp.float32
        )
    span, count = scores.shape
    block = min(SOFTMAX_ROWS, span)
    for first in range(0, span, block):
        rows = slice(first, first + block)
        row = first + lax.broadcasted_iota(jnp.int32, (block, count), 0)
        masked = jnp.where(token <= row, scores[rows], NEG)
        before, former = stats_of(rows)
        top = spread(jnp.max(masked, axis=1, keepdims=True))
        if before is not None:
            top = jnp.maximum(top, before)
        total = jnp.zeros_like(top)
        for c in range(0, count, LANES):
            part = jnp.exp2((masked[:, c : c + LANES] - top) * (SCALE * LOG2E))
            weights[rows, c : c + LANES] = part.astype(jnp.bfloat16)
            total = total + part
        total = spread(jnp.sum(total, axis=1, keepdims=True))
        factor = None
        if before is not None:
            factor = jnp.exp2((before - top) * (SCALE * LOG2E))
            total = former * factor + total
        yield rows, top, factor, total


def value_blocks(weights, keys):
    block = weights.shape[0] // 4
    for first in range(0, weights.shape[0], block):
        rows = slice(first, first + block)
        yield rows, jnp.dot(weights[rows], keys[:, :D_LAT], preferred_element_type=jnp.float32)


def early_kernel(
    tokens_ref, query_ref, own_ref, swap_ref, mixed_ref, top_ref, total_ref, scores, weights
):
    keys = joined_keys((own_ref, swap_ref))
    token = tokens_ref[0:1, : keys.shape[0]]
    for rows, top, _, total in fold_keys(
        query_ref, keys, token, lambda rows: (None, None), scores, weights
    ):
        top_ref[rows] = top
        total_ref[rows] = total
    for rows, mixed in value_blocks(weights, keys):
        mixed_ref[rows] = mixed


def middle_kernel(
    tokens_ref,
    query_ref,
    x_ref,
    y_ref,
    diagonal_ref,
    former_ref,
    before_ref,
    counted_ref,
    mixed_ref,
    top_ref,
    total_ref,
    scores,
    weights,
    factors,
):
    def stats_of(rows):
        return before_ref[rows], counted_ref[rows]

    keys = joined_keys((x_ref, y_ref, diagonal_ref))
    token = tokens_ref[1:2, : keys.shape[0]]
    for rows, top, factor, total in fold_keys(query_ref, keys, token, stats_of, scores, weights):
        top_ref[rows] = top
        total_ref[rows] = total
        factors[rows] = factor
    for rows, mixed in value_blocks(weights, keys):
        for c in range(0, D_LAT, LANES):
            part = slice(c, c + LANES)
            mixed_ref[rows, part] = former_ref[rows, part] * factors[rows] + mixed[:, part]


def late_kernel(
    tokens_ref,
    query_ref,
    x_ref,
    y_ref,
    diagonal_ref,
    former_ref,
    before_ref,
    counted_ref,
    out_ref,
    scores,
    weights,
    factors,
    scales,
    blocks,
    sems,
):
    def stats_of(rows):
        return before_ref[rows], counted_ref[rows]

    keys = joined_keys((x_ref, y_ref, diagonal_ref))
    token = tokens_ref[2:3, : keys.shape[0]]
    for rows, _, factor, total in fold_keys(query_ref, keys, token, stats_of, scores, weights):
        scale = 1.0 / total
        scales[rows] = scale
        factors[rows] = factor * scale
    stores = []
    for rows, mixed in value_blocks(weights, keys):
        for c in range(0, D_LAT, LANES):
            part = slice(c, c + LANES)
            blocks[rows, part] = (
                former_ref[rows, part] * factors[rows] + mixed[:, part] * scales[rows]
            ).astype(jnp.bfloat16)
        span = pl.ds(rows.start, rows.stop - rows.start)
        store = pltpu.make_async_copy(blocks.at[span], out_ref.at[span], sems.at[len(stores)])
        store.start()
        stores.append(store)
    for store in stores:
        store.wait()


def shards(n, prefill_query, prefill_latent, decode_query, cache, lengths, page_table):
    span = prefill_query.shape[0]
    rows, width = prefill_latent.shape
    heads = decode_query.shape[1]
    vmem = pl.BlockSpec(memory_space=pltpu.VMEM)
    hbm = pl.BlockSpec(memory_space=pltpu.HBM)
    params = pltpu.CompilerParams(vmem_limit_bytes=VMEM_LIMIT)

    packed = pl.pallas_call(
        decode_kernel,
        out_shape=jax.ShapeDtypeStruct((heads, 2 * REQ * GROUP, LANES), jnp.bfloat16),
        in_specs=[hbm] * 5,
        out_specs=vmem,
        scratch_shapes=[
            pltpu.SMEM(page_table.shape[::-1], jnp.int32),
            pltpu.SMEM(lengths.shape, jnp.int32),
            pltpu.VMEM(decode_query.shape, jnp.bfloat16),
            pltpu.VMEM((REQ, width, cache.shape[1]), jnp.bfloat16),
            pltpu.VMEM((rows, width), jnp.bfloat16),
            pltpu.VMEM((heads, 2 * REQ * GROUP, LANES), jnp.float32),
            pltpu.SemaphoreType.DMA((4 + REQ,)),
        ],
        compiler_params=pltpu.CompilerParams(vmem_limit_bytes=VMEM_MOST),
        cost_estimate=pl.CostEstimate(
            flops=4 * cache.size * heads, bytes_accessed=2 * cache.size, transcendentals=0
        ),
        name="decode_part",
    )(page_table.T, lengths, decode_query, jnp.swapaxes(cache, 1, 2), prefill_latent)
    groups = n // 8
    held = prefill_latent[None]
    mask = n // 2
    while mask >= 8:
        received = permute_mask(held, n, mask)
        held = join_slots(held, received, params)
        mask //= 2
    held_swap = permute_mask(held, n, 1)
    received, received_swap = [], []
    for number in range(1, 4):
        received.append(permute_mask(held, n, 2 * number))
    for number in range(1, 4):
        received_swap.append(permute_mask(received[number - 1], n, 1))

    moved = lax.all_to_all(packed, "ctx", split_axis=0, concat_axis=0, tiled=True)

    query = pl.pallas_call(
        turn_kernel,
        out_shape=jax.ShapeDtypeStruct((span, width), jnp.bfloat16),
        in_specs=[vmem],
        out_specs=vmem,
        compiler_params=params,
        cost_estimate=pl.CostEstimate(flops=0, bytes_accessed=4 * span * width, transcendentals=0),
        name="turn_query",
    )(jnp.transpose(prefill_query, (1, 2, 0)).reshape(width, span))
    tokens = pl.pallas_call(
        functools.partial(tokens_kernel, n, rows),
        out_shape=jax.ShapeDtypeStruct((3, 3 * groups * rows), jnp.int32),
        in_specs=[],
        out_specs=vmem,
        compiler_params=params,
        cost_estimate=pl.CostEstimate(flops=span, bytes_accessed=16, transcendentals=0),
        name="key_tokens",
    )()

    def cost(share):
        return pl.CostEstimate(
            flops=4 * span * span * width // share,
            bytes_accessed=4 * span * width,
            transcendentals=0,
        )

    sums = jax.ShapeDtypeStruct((span, D_LAT), jnp.float32)
    sums = (
        jax.ShapeDtypeStruct((span, D_LAT), jnp.float32),
        jax.ShapeDtypeStruct((span, LANES), jnp.float32),
        jax.ShapeDtypeStruct((span, LANES), jnp.float32),
    )

    def scratch(count):
        return [
            pltpu.VMEM((span, count * groups * rows), jnp.float32),
            pltpu.VMEM((span, count * groups * rows), jnp.bfloat16),
        ]

    factors = pltpu.VMEM((span, LANES), jnp.float32)
    early = pl.pallas_call(
        early_kernel,
        out_shape=sums,
        in_specs=[vmem] * 4,
        out_specs=(vmem,) * 3,
        scratch_shapes=scratch(2),
        compiler_params=params,
        cost_estimate=cost(4),
        name="prefill_early",
    )(tokens, query, held, held_swap)
    middle = pl.pallas_call(
        middle_kernel,
        out_shape=sums,
        in_specs=[vmem] * 8,
        out_specs=(vmem,) * 3,
        scratch_shapes=scratch(3) + [factors],
        compiler_params=params,
        cost_estimate=cost(2),
        name="prefill_middle",
    )(tokens, query, *received, *early)
    prefill_out = pl.pallas_call(
        late_kernel,
        out_shape=jax.ShapeDtypeStruct((span, D_LAT), jnp.bfloat16),
        in_specs=[vmem] * 8,
        out_specs=hbm,
        scratch_shapes=scratch(3)
        + [
            factors,
            factors,
            pltpu.VMEM((span, D_LAT), jnp.bfloat16),
            pltpu.SemaphoreType.DMA((4,)),
        ],
        compiler_params=params,
        cost_estimate=cost(2),
        name="prefill_late",
    )(tokens, query, *received_swap, *middle)
    decode_out = pl.pallas_call(
        merge_kernel,
        out_shape=jax.ShapeDtypeStruct((REQ, D_LAT), jnp.bfloat16),
        in_specs=[vmem],
        out_specs=vmem,
        compiler_params=params,
        cost_estimate=pl.CostEstimate(flops=moved.size, bytes_accessed=16, transcendentals=0),
        name="decode_merge",
    )(moved)
    return prefill_out.reshape(span, 1, D_LAT), decode_out.reshape(REQ, 1, D_LAT)


def solution(mesh):
    n = mesh.shape["ctx"]
    in_specs = (
        P("groups", "ctx", None),
        P(("groups", "ctx"), None),
        P("groups", None, None),
        P("groups", "ctx", None),
        P("groups"),
        P("groups", None),
    )
    out_specs = (P("groups", "ctx", None), P("groups", "ctx", None))

    def body(*args):
        return shards(n, *args)

    return jax.shard_map(
        body, mesh=mesh, in_specs=in_specs, out_specs=out_specs, check_vma=False
    )
```

```python
import functools

import jax
import jax.numpy as jnp
from jax import lax
from jax.experimental import pallas as pl
from jax.experimental.pallas import tpu as pltpu
from jax.sharding import PartitionSpec as P

D_LAT = 512
PAGE = 16
POOL = 16
REQ = 2
LANES = 128

SCALE = 192.0 ** (-0.5)
LOG2E = 1.4426950408889634
NEG = -1e30
SOFTMAX_ROWS = 32

VMEM_LIMIT = 12 << 20
VMEM_MOST = 60 << 20


def permute_mask(rows, n, mask):
    return lax.ppermute(rows, "ctx", [(i, i ^ mask) for i in range(n)])


def split_parts(value):
    parts = []
    for _ in range(3):
        part = value.astype(jnp.bfloat16).astype(jnp.float32)
        parts.append(part)
        value = value - part
    return parts


def pack_stats(top, total, lane):
    stats = jnp.zeros((top.shape[0], LANES), jnp.float32)
    for k, part in enumerate(split_parts(top) + split_parts(total)):
        stats = jnp.where(lane == k, part, stats)
    return stats


def spread_stats(packed):
    source = lax.broadcasted_iota(jnp.int32, (LANES, 2 * LANES), 0)
    target = lax.broadcasted_iota(jnp.int32, (LANES, 2 * LANES), 1)
    ones = jnp.where(source // 3 == target // LANES, 1.0, 0.0).astype(jnp.bfloat16)
    return jnp.dot(packed, ones, preferred_element_type=jnp.float32)


def decode_kernel(
    table_hbm,
    lengths_hbm,
    query_hbm,
    cache_hbm,
    latent_hbm,
    packed_ref,
    table_ref,
    lengths_ref,
    query_ref,
    cache_ref,
    latent_ref,
    rows_ref,
    sems,
):
    moves = [
        (cache_hbm.at[0], cache_ref.at[0]),
        (query_hbm, query_ref),
        (latent_hbm, latent_ref),
        (table_hbm, table_ref),
        (lengths_hbm, lengths_ref),
    ] + [(cache_hbm.at[r], cache_ref.at[r]) for r in range(1, REQ)]
    copies = [pltpu.make_async_copy(*move, sems.at[i]) for i, move in enumerate(moves)]
    for copy in copies:
        copy.start()

    device = lax.axis_index("ctx")
    rows = latent_ref.shape[0]
    length = cache_ref.shape[2]
    heads = query_ref.shape[1]
    first_page = (device * rows) // PAGE
    token = lax.broadcasted_iota(jnp.int32, (1, rows), 1)
    position = device * length + lax.broadcasted_iota(jnp.int32, (1, length), 1)
    lane = lax.broadcasted_iota(jnp.int32, (heads, LANES), 1)
    for copy in copies[1:5]:
        copy.wait()
    request = jnp.zeros((1, rows), jnp.int32)
    for k in range(max(1, rows // PAGE)):
        owner = table_ref[0, first_page + k]
        slot = table_ref[1, first_page + k]
        request = jnp.where(token // PAGE == k, lax.rem(owner * POOL + slot, REQ), request)
    latent = latent_ref[...]
    for r in range(REQ):
        query = query_ref[r]
        live = position < lengths_ref[r]
        mine = request == r
        page_scores = (
            lax.dot_general(
                query, latent, (((1,), (1,)), ((), ())), preferred_element_type=jnp.float32
            )
            * SCALE
        )
        copies[0 if r == 0 else 4 + r].wait()
        cache = cache_ref[r]
        cache_scores = jnp.dot(query, cache, preferred_element_type=jnp.float32) * SCALE
        top = jnp.maximum(
            jnp.max(jnp.where(live, cache_scores, NEG), axis=1, keepdims=True),
            jnp.max(jnp.where(mine, page_scores, NEG), axis=1, keepdims=True),
        )
        cache_weights = jnp.where(live, jnp.exp(cache_scores - top), 0.0)
        page_weights = jnp.where(mine, jnp.exp(page_scores - top), 0.0)
        total = jnp.sum(cache_weights, axis=1, keepdims=True) + jnp.sum(
            page_weights, axis=1, keepdims=True
        )
        mixed = lax.dot_general(
            cache_weights.astype(jnp.bfloat16),
            cache[:D_LAT],
            (((1,), (1,)), ((), ())),
            preferred_element_type=jnp.float32,
        ) + jnp.dot(
            page_weights.astype(jnp.bfloat16),
            latent[:, :D_LAT],
            preferred_element_type=jnp.float32,
        )
        stats = pack_stats(top, total, lane)
        rows_ref[:, r, :D_LAT] = mixed
        rows_ref[:, r, D_LAT:] = stats
    packed_ref[...] = rows_ref[...].astype(jnp.bfloat16)


def merge_kernel(moved_ref, decode_ref):
    senders = moved_ref.shape[0]
    stats = spread_stats(moved_ref[:, :, D_LAT:].reshape(-1, LANES))
    stats = stats.reshape(senders, REQ, 2 * LANES)
    tops = stats[:, :, :LANES]
    scales = jnp.exp(tops - jnp.max(tops, axis=0, keepdims=True))
    total = jnp.sum(stats[:, :, LANES:] * scales, axis=0)
    for c in range(0, D_LAT, LANES):
        mixed = jnp.sum(moved_ref[:, :, c : c + LANES].astype(jnp.float32) * scales, axis=0)
        decode_ref[:, c : c + LANES] = (mixed / total).astype(jnp.bfloat16)


def join_kernel(held_ref, received_ref, joined_ref):
    count = held_ref.shape[0]
    joined_ref[:count] = held_ref[...]
    joined_ref[count:] = received_ref[...]


def join_slots(held, received, params):
    vmem = pl.BlockSpec(memory_space=pltpu.VMEM)
    shape = (held.shape[0] + received.shape[0], *held.shape[1:])
    return pl.pallas_call(
        join_kernel,
        out_shape=jax.ShapeDtypeStruct(shape, held.dtype),
        in_specs=[vmem, vmem],
        out_specs=vmem,
        compiler_params=params,
        cost_estimate=pl.CostEstimate(flops=0, bytes_accessed=4 * held.size, transcendentals=0),
        name="join_slots",
    )(held, received)


def turn_kernel(turned_ref, query_ref):
    query_ref[...] = turned_ref[...].T


def tokens_kernel(n, rows, tokens_ref):
    device = lax.axis_index("ctx")
    shape = (1, tokens_ref.shape[1])
    groups = n // 8
    column = lax.broadcasted_iota(jnp.int32, shape, 1)
    slot = column // rows
    group = jnp.full_like(column, device // 8)
    bits = groups.bit_length() - 1
    for step in range(bits):
        group = group ^ (((slot >> step) & 1) << (bits - 1 - step))
    number = slot // groups
    for kernel, low in enumerate((number, 2 * (number + 1), 2 * (number + 1) + 1)):
        owner = group * 8 + ((device & 7) ^ low)
        tokens_ref[kernel : kernel + 1] = owner * rows + lax.rem(column, rows)


def spread(column):
    return jnp.broadcast_to(column, (column.shape[0], LANES))


def joined_keys(refs):
    return jnp.concatenate([ref[...].reshape(-1, ref.shape[2]) for ref in refs], axis=0)


def fold_keys(query_ref, keys, token, stats_of, scores, weights):
    cut = scores.shape[0] // 2
    for part in (slice(cut, None), slice(0, cut)):
        scores[part] = lax.dot_general(
            query_ref[part], keys, (((1,), (1,)), ((), ())), preferred_element_type=jnp.float32
        )
    span, count = scores.shape
    block = min(SOFTMAX_ROWS, span)
    for first in range(0, span, block):
        rows = slice(first, first + block)
        row = first + lax.broadcasted_iota(jnp.int32, (block, count), 0)
        masked = jnp.where(token <= row, scores[rows], NEG)
        before, former = stats_of(rows)
        top = spread(jnp.max(masked, axis=1, keepdims=True))
        if before is not None:
            top = jnp.maximum(top, before)
        total = jnp.zeros_like(top)
        for c in range(0, count, LANES):
            part = jnp.exp2((masked[:, c : c + LANES] - top) * (SCALE * LOG2E))
            weights[rows, c : c + LANES] = part.astype(jnp.bfloat16)
            total = total + part
        total = spread(jnp.sum(total, axis=1, keepdims=True))
        factor = None
        if before is not None:
            factor = jnp.exp2((before - top) * (SCALE * LOG2E))
            total = former * factor + total
        yield rows, top, factor, total


def value_blocks(weights, keys):
    block = weights.shape[0] // 4
    for first in range(0, weights.shape[0], block):
        rows = slice(first, first + block)
        yield rows, jnp.dot(weights[rows], keys[:, :D_LAT], preferred_element_type=jnp.float32)


def early_kernel(
    tokens_ref, query_ref, own_ref, swap_ref, mixed_ref, top_ref, total_ref, scores, weights
):
    keys = joined_keys((own_ref, swap_ref))
    token = tokens_ref[0:1, : keys.shape[0]]
    for rows, top, _, total in fold_keys(
        query_ref, keys, token, lambda rows: (None, None), scores, weights
    ):
        top_ref[rows] = top
        total_ref[rows] = total
    for rows, mixed in value_blocks(weights, keys):
        mixed_ref[rows] = mixed


def middle_kernel(
    tokens_ref,
    query_ref,
    x_ref,
    y_ref,
    diagonal_ref,
    former_ref,
    before_ref,
    counted_ref,
    mixed_ref,
    top_ref,
    total_ref,
    scores,
    weights,
    factors,
):
    def stats_of(rows):
        return before_ref[rows], counted_ref[rows]

    keys = joined_keys((x_ref, y_ref, diagonal_ref))
    token = tokens_ref[1:2, : keys.shape[0]]
    for rows, top, factor, total in fold_keys(query_ref, keys, token, stats_of, scores, weights):
        top_ref[rows] = top
        total_ref[rows] = total
        factors[rows] = factor
    for rows, mixed in value_blocks(weights, keys):
        for c in range(0, D_LAT, LANES):
            part = slice(c, c + LANES)
            mixed_ref[rows, part] = former_ref[rows, part] * factors[rows] + mixed[:, part]


def late_kernel(
    tokens_ref,
    query_ref,
    x_ref,
    y_ref,
    diagonal_ref,
    former_ref,
    before_ref,
    counted_ref,
    out_ref,
    scores,
    weights,
    factors,
    scales,
    blocks,
    sems,
):
    def stats_of(rows):
        return before_ref[rows], counted_ref[rows]

    keys = joined_keys((x_ref, y_ref, diagonal_ref))
    token = tokens_ref[2:3, : keys.shape[0]]
    for rows, _, factor, total in fold_keys(query_ref, keys, token, stats_of, scores, weights):
        scale = 1.0 / total
        scales[rows] = scale
        factors[rows] = factor * scale
    stores = []
    for rows, mixed in value_blocks(weights, keys):
        for c in range(0, D_LAT, LANES):
            part = slice(c, c + LANES)
            blocks[rows, part] = (
                former_ref[rows, part] * factors[rows] + mixed[:, part] * scales[rows]
            ).astype(jnp.bfloat16)
        span = pl.ds(rows.start, rows.stop - rows.start)
        store = pltpu.make_async_copy(blocks.at[span], out_ref.at[span], sems.at[len(stores)])
        store.start()
        stores.append(store)
    for store in stores:
        store.wait()


def shards(n, prefill_query, prefill_latent, decode_query, cache, lengths, page_table):
    span = prefill_query.shape[0]
    rows, width = prefill_latent.shape
    heads = decode_query.shape[1]
    vmem = pl.BlockSpec(memory_space=pltpu.VMEM)
    hbm = pl.BlockSpec(memory_space=pltpu.HBM)
    params = pltpu.CompilerParams(vmem_limit_bytes=VMEM_LIMIT)

    packed = pl.pallas_call(
        decode_kernel,
        out_shape=jax.ShapeDtypeStruct((heads, REQ, D_LAT + LANES), jnp.bfloat16),
        in_specs=[hbm] * 5,
        out_specs=vmem,
        scratch_shapes=[
            pltpu.SMEM(page_table.shape[::-1], jnp.int32),
            pltpu.SMEM(lengths.shape, jnp.int32),
            pltpu.VMEM(decode_query.shape, jnp.bfloat16),
            pltpu.VMEM((REQ, width, cache.shape[1]), jnp.bfloat16),
            pltpu.VMEM((rows, width), jnp.bfloat16),
            pltpu.VMEM((heads, REQ, D_LAT + LANES), jnp.float32),
            pltpu.SemaphoreType.DMA((4 + REQ,)),
        ],
        compiler_params=pltpu.CompilerParams(vmem_limit_bytes=VMEM_MOST),
        cost_estimate=pl.CostEstimate(
            flops=4 * cache.size * heads, bytes_accessed=2 * cache.size, transcendentals=0
        ),
        name="decode_part",
    )(page_table.T, lengths, decode_query, jnp.swapaxes(cache, 1, 2), prefill_latent)
    groups = n // 8
    held = prefill_latent[None]
    mask = n // 2
    while mask >= 8:
        received = permute_mask(held, n, mask)
        held = join_slots(held, received, params)
        mask //= 2
    held_swap = permute_mask(held, n, 1)
    received, received_swap = [], []
    for number in range(1, 4):
        received.append(permute_mask(held, n, 2 * number))
    for number in range(1, 4):
        received_swap.append(permute_mask(received[number - 1], n, 1))

    moved = lax.all_to_all(packed, "ctx", split_axis=0, concat_axis=0, tiled=True)

    query = pl.pallas_call(
        turn_kernel,
        out_shape=jax.ShapeDtypeStruct((span, width), jnp.bfloat16),
        in_specs=[vmem],
        out_specs=vmem,
        compiler_params=params,
        cost_estimate=pl.CostEstimate(flops=0, bytes_accessed=4 * span * width, transcendentals=0),
        name="turn_query",
    )(jnp.transpose(prefill_query, (1, 2, 0)).reshape(width, span))
    tokens = pl.pallas_call(
        functools.partial(tokens_kernel, n, rows),
        out_shape=jax.ShapeDtypeStruct((3, 3 * groups * rows), jnp.int32),
        in_specs=[],
        out_specs=vmem,
        compiler_params=params,
        cost_estimate=pl.CostEstimate(flops=span, bytes_accessed=16, transcendentals=0),
        name="key_tokens",
    )()

    def cost(share):
        return pl.CostEstimate(
            flops=4 * span * span * width // share,
            bytes_accessed=4 * span * width,
            transcendentals=0,
        )

    sums = jax.ShapeDtypeStruct((span, D_LAT), jnp.float32)
    sums = (
        jax.ShapeDtypeStruct((span, D_LAT), jnp.float32),
        jax.ShapeDtypeStruct((span, LANES), jnp.float32),
        jax.ShapeDtypeStruct((span, LANES), jnp.float32),
    )

    def scratch(count):
        return [
            pltpu.VMEM((span, count * groups * rows), jnp.float32),
            pltpu.VMEM((span, count * groups * rows), jnp.bfloat16),
        ]

    factors = pltpu.VMEM((span, LANES), jnp.float32)
    early = pl.pallas_call(
        early_kernel,
        out_shape=sums,
        in_specs=[vmem] * 4,
        out_specs=(vmem,) * 3,
        scratch_shapes=scratch(2),
        compiler_params=params,
        cost_estimate=cost(4),
        name="prefill_early",
    )(tokens, query, held, held_swap)
    middle = pl.pallas_call(
        middle_kernel,
        out_shape=sums,
        in_specs=[vmem] * 8,
        out_specs=(vmem,) * 3,
        scratch_shapes=scratch(3) + [factors],
        compiler_params=params,
        cost_estimate=cost(2),
        name="prefill_middle",
    )(tokens, query, *received, *early)
    prefill_out = pl.pallas_call(
        late_kernel,
        out_shape=jax.ShapeDtypeStruct((span, D_LAT), jnp.bfloat16),
        in_specs=[vmem] * 8,
        out_specs=hbm,
        scratch_shapes=scratch(3)
        + [
            factors,
            factors,
            pltpu.VMEM((span, D_LAT), jnp.bfloat16),
            pltpu.SemaphoreType.DMA((4,)),
        ],
        compiler_params=params,
        cost_estimate=cost(2),
        name="prefill_late",
    )(tokens, query, *received_swap, *middle)
    decode_out = pl.pallas_call(
        merge_kernel,
        out_shape=jax.ShapeDtypeStruct((REQ, D_LAT), jnp.bfloat16),
        in_specs=[vmem],
        out_specs=vmem,
        compiler_params=params,
        cost_estimate=pl.CostEstimate(flops=moved.size, bytes_accessed=16, transcendentals=0),
        name="decode_merge",
    )(moved)
    return prefill_out.reshape(span, 1, D_LAT), decode_out.reshape(REQ, 1, D_LAT)


def solution(mesh):
    n = mesh.shape["ctx"]
    in_specs = (
        P("groups", "ctx", None),
        P(("groups", "ctx"), None),
        P("groups", None, None),
        P("groups", "ctx", None),
        P("groups"),
        P("groups", None),
    )
    out_specs = (P("groups", "ctx", None), P("groups", "ctx", None))

    def body(*args):
        return shards(n, *args)

    return jax.shard_map(
        body, mesh=mesh, in_specs=in_specs, out_specs=out_specs, check_vma=False
    )
```
